32 devices in a mesh: seq: 8 (over z, y), mp: 4 (over x, core).
Axes of the slice: x: 2, y: 2, z: 4, core: 2. Of those that a mesh axis runs over, the one named last changes fastest.
Arguments:
- tokens: bfloat16 [16384, 2048], P('seq'), may hold values from -6 to 6
- w_proj: bfloat16 [2048, 4, 2048], P(None, None, 'mp')
- gain: float32 [2048], P('mp'), may hold values from 0.25 to 1.75
- level_codes: int32 [9, 16, 16384], P(None, 'mp', 'seq'), may hold values from 0 to 255
- w_codes: int32 [2048, 2048], P('mp'), may hold values from 40 to 199, as said below
- block_exponent: int32 [16, 16], P('mp'), may hold values from -7 to -5
Outputs:
- mixed: bfloat16 [16384, 2048], P(('seq', 'mp'))
The draws below stay inside these ranges and needn't reach their ends.
Inputs may be any that keep to these rules, and one draw needn't show every extreme that they name: `w_codes`: each code is 128 s + 8 e + m with s of 0 or 1, e from 5 to 8 and m from 0 to 7.
All inputs are finite; a program needn't handle non-finite values.
Results may differ from the reference program's by a relative error of at most 0.015.
Values may be sent and summed in bfloat16 or wider, within the bound.
A program may use at most 128 MiB of HBM per device.

```python
import math
import jax
import jax.numpy as jnp
from jax import lax

D = 2048
HEADS = 16
HEAD_DIM = 128
STRETCH = 64
BLOCK = 128
HD = 2048
TOKENS = 16384
LEVELS = 9
N_MP = 4


def draw_w_proj(key, part):
    first, second = jax.random.split(jax.random.fold_in(key, 11), 2)
    width = HEADS * HEAD_DIM
    column_scale = jnp.exp(jax.random.uniform(first, (1, 4, width), jnp.float32, math.log(0.3), math.log(3.0)))
    base = jax.random.normal(second, (D, 4, width), jnp.float32)
    return (base * column_scale / math.sqrt(D)).astype(jnp.bfloat16)


def draw_w_codes(key, part):
    first, second, third = jax.random.split(jax.random.fold_in(key, 23), 3)
    width = HEADS * HEAD_DIM
    negative = jax.random.randint(first, (width, D), 0, 2, jnp.int32)
    exponent = jax.random.randint(second, (width, D), 5, 9, jnp.int32)
    mantissa = jax.random.randint(third, (width, D), 0, 8, jnp.int32)
    return 128 * negative + 8 * exponent + mantissa


def plant(values, rng, least, high):
    longest = values.shape.index(max(values.shape))
    spots = []
    for shift in (0, 1):
        where = [jax.random.randint(jax.random.fold_in(rng, axis), (), 0, length) for axis, length in enumerate(values.shape)]
        where[longest] = (where[longest] + shift) % values.shape[longest]
        spots.append(tuple(where))
    return values.at[spots[0]].set(least).at[spots[1]].set(high)


def block_scale(key, dims, cuts, smallest, largest):
    loudness = 1.0
    for axis_at, blocks in cuts:
        draws = jax.random.uniform(jax.random.fold_in(jax.random.fold_in(key, 6), axis_at), (blocks,), jnp.float32, smallest / len(cuts), largest / len(cuts))
        loudness = loudness * jnp.repeat(jnp.exp(draws), dims[axis_at] // blocks).reshape((-1,) + (1,) * (len(dims) - 1 - axis_at))
    return loudness


def gaussian(rng, extent, spread, bound, cuts=(), dtype=jnp.bfloat16):
    level = block_scale(rng, extent, cuts, -0.22, 0.18) if cuts else 1.0
    entries = jax.random.normal(rng, extent, jnp.float32) * spread * level
    return jnp.minimum(jnp.maximum(entries, -bound), bound).astype(dtype)


def setup_inputs(seed: int = 0) -> dict:
    key_list = jax.random.split(jax.random.key(seed), 7)
    tokens = gaussian(key_list[0], (TOKENS, D), 1.0, 6.0, ((0, 8),))
    w_proj = draw_w_proj(jax.random.fold_in(key_list[6], 71), 0)
    gain = jnp.clip(1.0 + 0.15 * jax.random.normal(key_list[2], (HD,), jnp.float32), 0.25, 1.75)
    level_codes = plant(jax.random.randint(key_list[3], (LEVELS, HEADS, TOKENS), 0, 256), jax.random.fold_in(key_list[3], 1), 0, 255).astype(jnp.int32)
    w_codes = draw_w_codes(jax.random.fold_in(key_list[6], 71), 0)
    block_exponent = plant(jax.random.randint(key_list[5], (HD // BLOCK, D // BLOCK), -7, -4), jax.random.fold_in(key_list[5], 1), -7, (-4) - 1).astype(jnp.int32)
    return dict(tokens=tokens, w_proj=w_proj, gain=gain, level_codes=level_codes, w_codes=w_codes, block_exponent=block_exponent)


def power_of_two(field, bits):
    result = jnp.ones(field.shape, jnp.float32)
    for bit in range(bits):
        result = result * jnp.where(field // 2 ** bit % 2 == 1, jnp.float32(2.0 ** 2 ** bit), jnp.float32(1.0))
    return result

def decode_weight(codes, exponents, block):
    negative = codes // 128
    exponent = codes // 8 % 16
    mantissa = codes % 8
    magnitude = (8 + mantissa).astype(jnp.float32) * (1 - 2 * negative).astype(jnp.float32)
    magnitude = magnitude * power_of_two(exponent, 4) * jnp.float32(2.0 ** (-10))
    scales = power_of_two(exponents + 16, 5) * jnp.float32(2.0 ** (-16))
    rows, columns = codes.shape
    shaped = magnitude.reshape(rows // block, block, columns // block, block) * scales[:, None, :, None]
    return shaped.reshape(rows, columns).astype(jnp.bfloat16)

def head_mix(inputs):
    query, keys, values, level_weight = inputs
    stretches = TOKENS // STRETCH
    query_blocks = query.reshape(stretches, STRETCH, HEAD_DIM)
    key_blocks = keys.reshape(stretches, STRETCH, HEAD_DIM).astype(jnp.float32)
    value_blocks = values.reshape(stretches, STRETCH, HEAD_DIM).astype(jnp.float32)
    scores = jnp.einsum('ntd,nsd->nts', query_blocks.astype(jnp.float32), key_blocks)
    causal = jnp.tril(jnp.ones((STRETCH, STRETCH), bool))
    weights = (jnp.where(causal[None], scores, 0.0) * (1.0 / math.sqrt(HEAD_DIM * STRETCH))).astype(jnp.bfloat16)
    local = jnp.einsum('nts,nsd->ntd', weights.astype(jnp.float32), value_blocks)
    total = level_weight[0].reshape(stretches, STRETCH)[:, :, None] * local
    blocks = jnp.einsum('ntd,nte->nde', key_blocks, value_blocks)
    for level in range(LEVELS - 1):
        count = stretches >> level + 1
        span = STRETCH << level
        pairs = blocks.reshape(count, 2, HEAD_DIM, HEAD_DIM)
        sibling = pairs[:, 0].astype(jnp.bfloat16)
        second = query_blocks.reshape(count, 2, span, HEAD_DIM)[:, 1]
        term = jnp.einsum('ptd,pde->pte', second.astype(jnp.float32), sibling.astype(jnp.float32))
        term = term * (1.0 / math.sqrt(HEAD_DIM * span))
        weight_second = level_weight[level + 1].reshape(count, 2, span)[:, 1]
        placed = jnp.stack([jnp.zeros_like(term), weight_second[:, :, None] * term], 1)
        total = total + placed.reshape(stretches, STRETCH, HEAD_DIM)
        blocks = pairs[:, 0] + pairs[:, 1]
    return total.reshape(TOKENS, HEAD_DIM)

def reference(tokens, w_proj, gain, level_codes, w_codes, block_exponent):
    width = HEADS * HEAD_DIM
    projected = jnp.dot(tokens, w_proj.reshape(D, 4 * width), preferred_element_type=jnp.float32)
    projected = projected.reshape(TOKENS, 4, HEADS, HEAD_DIM)
    query = projected[:, 0].astype(jnp.bfloat16).transpose(1, 0, 2)
    keys = projected[:, 1].astype(jnp.bfloat16).transpose(1, 0, 2)
    values = projected[:, 2].astype(jnp.bfloat16).transpose(1, 0, 2)
    gate = jax.nn.silu(projected[:, 3].reshape(TOKENS, width))
    level_weight = (level_codes.astype(jnp.float32) / 128.0).transpose(1, 0, 2)
    memory = lax.map(head_mix, (query, keys, values, level_weight)).transpose(1, 0, 2)
    normed = memory * lax.rsqrt(lax.optimization_barrier(jnp.mean(memory * memory, axis=-1, keepdims=True)) + 1e-06)
    attended = (normed.reshape(TOKENS, width) * gain * gate).astype(jnp.bfloat16)
    weight = decode_weight(w_codes, block_exponent, BLOCK)
    group = width // N_MP
    mixed = jnp.zeros((TOKENS, D), jnp.float32)
    for member in range(N_MP):
        partial_value = jnp.dot(attended[:, member * group:(member + 1) * group], weight[member * group:(member + 1) * group], preferred_element_type=jnp.float32).astype(jnp.bfloat16)
        partial_value = lax.optimization_barrier(partial_value)
        mixed = mixed + partial_value.astype(jnp.float32)
    return mixed.astype(jnp.bfloat16)
```

```python
import functools
import math

import jax
import jax.numpy as jnp
from jax import lax
from jax.experimental import pallas as pl
from jax.experimental.pallas import tpu as pltpu
from jax.sharding import PartitionSpec as P

HEAD_DIM = 128
STRETCH = 64
BLOCK = 128
CORES = 2
QB = 256
QUARTERS = 4
CHUNKS = 4
MESH = pl.DeviceIdType.MESH
F32 = jnp.float32
BF16 = jnp.bfloat16


def dot(a, b):
    return jnp.dot(a, b, preferred_element_type=F32)


def dot_nt(a, b):
    return lax.dot_general(a, b, (((1,), (1,)), ((), ())), preferred_element_type=F32)


def dot_tn(a, b):
    return lax.dot_general(a, b, (((0,), (0,)), ((), ())), preferred_element_type=F32)


def kernel(
    cfg,
    tok_hbm, w_hbm, codes_hbm, gain_hbm, lw_hbm, scale_ref,
    out_hbm,
    tok, wstage, cstage, wfull, kv, q, gate, att, attr, local, tot, snd, rcv, masks, acc, outv,
    lw_ref, gain_ref,
    tok_sem, w_sem, c_sem, in_sem, out_sem, ws_sem, wr_sem, as_sem, ar_sem, ss_sem, sr_sem,
    *wh,
):
    groups, seq_bits, block_bits, in_bits, factors = cfg
    rows_all, depth = tok.shape
    pairs = len(wh)
    heads, width = tot.shape[0], att.shape[1]
    hp = heads // pairs
    pw = hp * HEAD_DIM
    rows = rows_all // groups
    chips = groups // CORES
    n_parts = rows // QB
    n_b = rows_all // QB
    seq = lax.axis_index("seq")
    mp = lax.axis_index("mp")
    x = mp // CORES
    c = mp % CORES
    bit0 = seq % 2
    bit1 = (seq // 2) % 2

    def peer(ix, kc):
        return ((x + ix) % chips) * CORES + (c + kc) % CORES

    def source(ix, kc):
        return ((x - ix + chips) % chips) * CORES + (c - kc + CORES) % CORES

    def seq_peer(j):
        bit = (seq // 2**j) % 2
        return seq + 2**j - bit * 2 ** (j + 1)

    mine = bit1 * 2 + bit0
    over0 = bit1 * 2 + 1 - bit0
    over1 = (1 - bit1) * 2 + bit0
    over01 = (1 - bit1) * 2 + 1 - bit0

    crows = width // QUARTERS
    n_t = 4
    tb = rows_all // n_t
    wrows = depth // n_t

    def code_piece(i):
        return (mine + i) % QUARTERS

    def c_copy(i):
        at = pl.ds(pl.multiple_of(code_piece(i) * crows, crows), crows)
        return pltpu.make_async_copy(codes_hbm.at[at], cstage.at[i], c_sem.at[i])

    def w_copy(h, i):
        at = pl.ds(i * wrows, wrows)
        cols = pl.ds(h * pw, pw)
        return pltpu.make_async_copy(
            w_hbm.at[at, :, cols], wstage.at[h % 2, at], w_sem.at[h % 2, i]
        )

    def tok_copy(i):
        at = pl.ds(pl.multiple_of(i * tb, tb), tb)
        return pltpu.make_async_copy(tok_hbm.at[at], tok.at[at], tok_sem.at[i])

    c_copy(0).start()
    for i in range(n_t):
        w_copy(0, i).start()
    tok_copy(0).start()
    tok_copy(1).start()
    if pairs > 1:
        for i in range(n_t):
            w_copy(1, i).start()
    tok_copy(2).start()
    tok_copy(3).start()
    for i in range(1, QUARTERS):
        c_copy(i).start()
    lw_copy = pltpu.make_async_copy(lw_hbm, lw_ref, in_sem.at[0])
    gain_copy = pltpu.make_async_copy(gain_hbm, gain_ref, in_sem.at[1])
    lw_copy.start()
    gain_copy.start()

    barrier = pltpu.get_barrier_semaphore()
    for r in range(1, groups):
        pl.semaphore_signal(
            barrier, inc=1, device_id=(seq, peer(r // CORES, r % CORES)), device_id_type=MESH
        )
    for j in range(seq_bits):
        pl.semaphore_signal(barrier, inc=1, device_id=(seq_peer(j), mp), device_id_type=MESH)

    def decode(i, start, size):
        piece = code_piece(i)
        codes = cstage[i, pl.ds(start, size)]
        whole = ((codes & 7) | 8) << ((codes >> 3) & 15)
        value = whole.astype(F32)
        value = jnp.where(codes >= 128, -value, value)
        at = pl.ds(pl.multiple_of(piece * crows + start, 16), size)
        block = piece * crows // BLOCK
        for k in range(depth // BLOCK):
            scale = jnp.left_shift(jnp.int32(1), scale_ref[block, k] + 16).astype(F32) * 2.0**-26
            cols = slice(k * BLOCK, (k + 1) * BLOCK)
            wfull[mp, at, cols] = (value[:, cols] * scale).astype(BF16)

    def relayout(p, start, size):
        at = pl.ds(pl.multiple_of(start, size), size)
        piece = jnp.swapaxes(wstage[p % 2, at], 0, 1)
        wh[p][0, at, :pw] = piece[1]
        wh[p][0, at, pw:] = piece[2]
        wh[p][1, at, :pw] = piece[0]
        wh[p][1, at, pw:] = piece[3]

    csize = crows // CHUNKS

    def w_send(k, shard, start, size, seq_to, mp_to):
        at = pl.ds(pl.multiple_of(start, 16), size)
        return pltpu.make_async_remote_copy(
            src_ref=wfull.at[shard, at], dst_ref=wfull.at[shard, at],
            send_sem=ws_sem.at[k], recv_sem=wr_sem.at[k],
            device_id=(seq_to, mp_to), device_id_type=MESH,
        )

    n_x = chips - 1
    per = 4 * CHUNKS + 4

    def slot(ix, kind, ch):
        return (ix - 1) * per + kind * CHUNKS + ch

    def x_part(ix, ch, shard):
        return w_send(slot(ix, 0, ch), shard, mine * crows + ch * csize, csize, seq, peer(ix, 0))

    def y_part(ix, ch, quarter):
        at = quarter * crows + ch * csize
        return w_send(slot(ix, 1, ch), source(ix, 0), at, csize, seq_peer(0), mp)

    def z_part(ix, ch, quarter):
        at = quarter * crows + ch * csize
        return w_send(slot(ix, 2, ch), source(ix, 0), at, csize, seq_peer(1), mp)

    def d_part(ix, ch, quarter):
        at = quarter * crows + ch * csize
        return w_send(slot(ix, 3, ch), source(ix, 0), at, csize, seq_peer(0), mp)

    def core_part(ix, n, kc):
        quarter = (mine, over0, over1, over01)[n]
        k = slot(ix, 4, 0) + n
        return w_send(k, source(ix, kc), quarter * crows, crows, seq, peer(0, 1))

    def own_part(shard):
        return w_send(n_x * per, shard, 0, width, seq, peer(0, 1))

    remote = range(1, chips)

    def core_send(n):
        for ix in remote:
            core_part(ix, n, 0).start()

    def x_relay(ch):
        for ix in remote:
            x_part(ix, ch, source(ix, 0)).wait_recv()
            y_part(ix, ch, mine).start()
        if ch == CHUNKS - 1:
            core_send(0)

    def z_start(ch):
        for ix in remote:
            z_part(ix, ch, mine).start()

    def z_relay(ch):
        for ix in remote:
            z_part(ix, ch, over1).wait_recv()
            d_part(ix, ch, over1).start()
        if ch == CHUNKS - 1:
            core_send(2)

    def y_done():
        for ix in remote:
            for ch in range(CHUNKS):
                y_part(ix, ch, over0).wait_recv()
        core_send(1)

    def d_done():
        for ix in remote:
            for ch in range(CHUNKS):
                d_part(ix, ch, over01).wait_recv()
        core_send(3)

    def part_of(h, which):
        lo = which * pw + h % hp * HEAD_DIM
        return slice(lo, lo + HEAD_DIM)

    def states(h):
        level = []
        for b in range(n_b):
            at = pl.ds(b * QB, QB)
            level.append(dot_tn(kv[h // hp, at, part_of(h, 1)], kv[h // hp, at, part_of(h, 0)]))
        base = 0
        while len(level) > 1:
            for b, state in enumerate(level):
                local[base + b, h] = state.astype(BF16)
            base += len(level)
            level = [level[2 * b] + level[2 * b + 1] for b in range(len(level) // 2)]
        tot[h] = level[0]
        snd[0, h] = level[0].astype(BF16)

    def s_send(j, h):
        return pltpu.make_async_remote_copy(
            src_ref=snd.at[j, h], dst_ref=rcv.at[j, h],
            send_sem=ss_sem.at[j, h], recv_sem=sr_sem.at[j, h],
            device_id=(seq_peer(j), mp), device_id_type=MESH,
        )

    progress = [0] * heads

    def exchange(h):
        j = progress[h]
        s_send(j, h).wait_recv()
        if j + 1 < seq_bits:
            total = tot[h] + rcv[j, h].astype(F32)
            tot[h] = total
            snd[j + 1, h] = total.astype(BF16)
            s_send(j + 1, h).start()
        progress[h] += 1

    def advance(p, upto):
        for h in range(p * hp, (p + 1) * hp) if p < pairs else ():
            if progress[h] < min(upto, seq_bits - 1):
                exchange(h)

    def complete(h):
        while progress[h] < seq_bits:
            exchange(h)

    def query(p, first, last, after=None):
        @pl.loop(first, last)
        def _(step):
            r = groups - 1 - step
            owner = peer(r // CORES, r % CORES)
            at = pl.ds(pl.multiple_of(owner * rows, rows), rows)
            both = dot(tok[at, :], wh[p][1])
            q[p, at, :] = both[:, :pw].astype(BF16)
            g = both[:, pw:]
            gain = gain_ref[:, p * pw : (p + 1) * pw]
            gate[p, at, :] = g / (1.0 + jnp.exp(-g)) * gain
            if after:
                pl.when(step == first)(after)

    def a_send(r, target, part, h):
        at = pl.ds(pl.multiple_of(target * rows + part * QB, QB), QB)
        to = pl.ds(pl.multiple_of(part * QB, QB), QB)
        cols = pl.ds(h * HEAD_DIM, HEAD_DIM)
        k = (r * n_parts + part) * heads + h
        return pltpu.make_async_remote_copy(
            src_ref=att.at[at, cols], dst_ref=attr.at[mp, to, cols],
            send_sem=as_sem.at[k], recv_sem=ar_sem.at[k],
            device_id=(seq, target), device_id_type=MESH,
        )

    def a_wait(r, part, h):
        src = source(r // CORES, r % CORES)
        to = pl.ds(part * QB, QB)
        cols = pl.ds(h * HEAD_DIM, HEAD_DIM)
        k = (r * n_parts + part) * heads + h
        pltpu.make_async_remote_copy(
            src_ref=attr.at[src, to, cols], dst_ref=attr.at[src, to, cols],
            send_sem=as_sem.at[k], recv_sem=ar_sem.at[k],
            device_id=(seq, src), device_id_type=MESH,
        ).wait_recv()

    unit = 2
    hb = QB // 2
    n_in = 1 + in_bits

    def attend_block(h, b):
        cols = slice(h * HEAD_DIM, (h + 1) * HEAD_DIM)
        at = pl.ds(pl.multiple_of(b * QB, QB), QB)
        qh = q[h // hp, at, part_of(h, 0)]

        def weight(level):
            return lw_ref[level, h : h + 1, at].astype(F32) * factors[level]

        scores = dot_nt(kv[h // hp, at, part_of(h, 0)], qh)

        def corner(lo):
            side = slice(lo, lo + hb)
            mix = weight(0)[:, side] * masks[0]
            for j in range(in_bits - 1):
                mix = mix + weight(1 + j)[:, side] * masks[1 + j]
            return (scores[side, side] * mix).astype(BF16)

        upper = (scores[:hb, hb:] * weight(in_bits)[:, hb:]).astype(BF16)
        probs = jnp.concatenate(
            [
                jnp.concatenate([corner(0), upper], 1),
                jnp.concatenate([jnp.zeros((hb, hb), BF16), corner(hb)], 1),
            ],
            0,
        )
        qt = qh.astype(F32).T
        left = []
        right = []
        base = 0
        for j in range(block_bits):
            node = b // 2**j
            bit = node % 2
            right.append((qt * (weight(n_in + j) * bit.astype(F32))).astype(BF16))
            left.append(local[base + node - bit, h])
            base += n_b >> j
        for j in range(seq_bits):
            bit = (seq // 2**j) % 2
            right.append((qt * (weight(n_in + block_bits + j) * bit.astype(F32))).astype(BF16))
            left.append(rcv[j, h])
        memory = dot_tn(kv[h // hp, at, part_of(h, 1)], probs) + dot(
            jnp.concatenate(left, 1), jnp.concatenate(right, 0)
        )
        mean = jnp.mean(memory * memory, axis=0, keepdims=True)
        normed = (memory * lax.rsqrt(mean + 1e-06)).T
        att[at, cols] = (normed * gate[h // hp, at, part_of(h, 0)]).astype(BF16)

    def attend(p, first, last):
        pair = range(p * hp, (p + 1) * hp)
        span = last - first

        @pl.loop(0, n_parts * span // unit)
        def _(i):
            todo = []
            for k in range(unit):
                n = i * unit + k
                r = groups - 1 - first - n % span
                todo.append((r, peer(r // CORES, r % CORES), n // span))
            for r, owner, part in todo:
                for h in pair:
                    attend_block(h, owner * n_parts + part)
            for r, owner, part in todo:
                @pl.when(r > 0)
                def _():
                    for h in pair:
                        a_send(r, owner, part, h).start()

    nb = min(512, depth)

    c_copy(0).wait()
    decode(0, 0, crows)
    pl.semaphore_wait(barrier, groups - 1 + seq_bits)
    for ch in range(CHUNKS):
        for ix in remote:
            x_part(ix, ch, mp).start()
    for i in range(n_t):
        w_copy(0, i).wait()
        relayout(0, i * wrows, wrows)

    t = lax.broadcasted_iota(jnp.int32, (hb, hb), 1)
    s = lax.broadcasted_iota(jnp.int32, (hb, hb), 0)
    tc = t // STRETCH
    sc = s // STRETCH
    masks[0] = jnp.where((tc == sc) & (s <= t), 1.0, 0.0).astype(F32)
    for j in range(in_bits - 1):
        hit = ((tc // 2**j) % 2 == 1) & (sc // 2**j == tc // 2**j - 1)
        masks[j + 1] = jnp.where(hit, 1.0, 0.0).astype(F32)

    moves = {}
    for ch in range(CHUNKS):
        moves["x", ch] = functools.partial(x_relay, ch)
    for ch in range(CHUNKS):
        moves["z", ch] = functools.partial(z_start, ch)
    moves["y", 0] = y_done
    for ch in range(CHUNKS):
        moves["zr", ch] = functools.partial(z_relay, ch)
    moves["d", 0] = d_done

    def move(name, ch=0):
        step = moves.pop((name, ch), None)
        if step:
            step()

    half = n_t // 2
    sub = crows // n_t
    for p in range(pairs):
        last = p + 1 == pairs
        now = range(1, QUARTERS) if last else ()
        for i in now:
            c_copy(i).wait()

        def project(i):
            at = pl.ds(pl.multiple_of(i * tb, tb), tb)
            kv[p, at, :] = dot(tok[at, :], wh[p][0]).astype(BF16)
            for piece in now:
                decode(piece, i * sub, sub)

        @pl.loop(0, half)
        def _(i):
            if p == 0:
                tok_copy(i).wait()
            project(i)

        if p > 0:
            move("x", 1)
        if not last:
            for i in range(n_t):
                w_copy(p + 1, i).wait()

        @pl.loop(half, n_t)
        def _(i):
            if p == 0:
                tok_copy(i).wait()
            project(i)
            if not last:
                for k in range(4):
                    relayout(p + 1, (i - half) * 2 * wrows + k * wrows // 2, wrows // 2)
            if p > 0:
                @pl.when(i == half)
                def _():
                    advance(p - 1, 1)

        for h in range(p * hp, (p + 1) * hp):
            states(h)
            s_send(0, h).start()
        if p == 0:
            move("x", 0)
            move("z", 0)
        else:
            move("x", 2)
            move("x", 3)
    own_part(mp).start()

    lw_copy.wait()
    gain_copy.wait()
    n_far = groups - CORES
    query(0, 0, n_far, functools.partial(advance, 0, 2))
    if pairs > 1:
        query(1, 0, n_far, functools.partial(advance, 1, 1))
        move("z", 1)
    for h in range(hp):
        complete(h)
    attend(0, 0, n_far)
    advance(1, 2)
    for ch in range(CHUNKS):
        move("x", ch)
        move("z", ch)
    query(0, n_far, groups)
    move("y")
    move("zr", 0)
    if pairs > 1:
        query(1, n_far, groups)
        for h in range(hp, heads):
            complete(h)
        attend(1, 0, n_far)
    move("zr", 1)
    attend(0, n_far, groups)
    move("zr", 2)
    if pairs > 1:
        attend(1, n_far, groups)
    move("zr", 3)

    own = pl.ds(pl.multiple_of(mp * rows, rows), rows)
    partner = source(0, 1)
    for part in range(n_parts):
        for h in range(heads):
            a_wait(1, part, h)
    own_part(partner).wait_recv()

    @pl.loop(0, depth // nb)
    def _(i):
        cols = pl.ds(pl.multiple_of(i * nb, nb), nb)
        acc[:, cols] = dot(att[own, :], wfull[mp, :, cols]) + dot(
            attr[partner], wfull[partner, :, cols]
        )

    for name, ch in list(moves):
        move(name, ch)
    for ix in remote:
        for n in range(4):
            core_part(ix, n, 1).wait_recv()

    early = heads // 2
    cut = early * HEAD_DIM
    far = range(CORES, groups)
    for r in far:
        for part in range(n_parts):
            for h in range(early):
                a_wait(r, part, h)

    def far_sum(at, ks, cols):
        value = acc[at, cols]
        for r in far:
            src = source(r // CORES, r % CORES)
            value = value + dot(attr[src, at, ks], wfull[src, ks, cols])
        return value

    @pl.loop(0, depth // nb)
    def _(i):
        cols = pl.ds(pl.multiple_of(i * nb, nb), nb)
        acc[:, cols] = far_sum(slice(0, rows), slice(0, cut), cols)

    def out_copy(part):
        at = pl.ds(part * QB, QB)
        return pltpu.make_async_copy(outv.at[at], out_hbm.at[at], out_sem.at[part])

    for part in range(n_parts):
        for r in far:
            for h in range(early, heads):
                a_wait(r, part, h)
        at = slice(part * QB, (part + 1) * QB)

        @pl.loop(0, depth // nb)
        def _(i):
            cols = pl.ds(pl.multiple_of(i * nb, nb), nb)
            outv[at, cols] = far_sum(at, slice(cut, width), cols).astype(BF16)

        out_copy(part).start()

    own_part(mp).wait_send()
    for ix in remote:
        for ch in range(CHUNKS):
            x_part(ix, ch, mp).wait_send()
            y_part(ix, ch, mine).wait_send()
            z_part(ix, ch, mine).wait_send()
            d_part(ix, ch, over1).wait_send()
        for n in range(4):
            core_part(ix, n, 0).wait_send()
    for j in range(seq_bits):
        for h in range(heads):
            s_send(j, h).wait_send()
    for r in range(1, groups):
        for part in range(n_parts):
            for h in range(heads):
                a_send(r, peer(r // CORES, r % CORES), part, h).wait_send()
    for part in range(n_parts):
        out_copy(part).wait()


def body(tokens, w_proj, gain, level_codes, w_codes, block_exponent):
    rows_all, depth = tokens.shape
    width = w_proj.shape[2]
    heads = width // HEAD_DIM
    pw = 2 * HEAD_DIM
    pairs = width // pw
    groups = lax.axis_size("mp")
    seq_size = lax.axis_size("seq")
    seq_bits = seq_size.bit_length() - 1
    stretch_bits = (rows_all // STRETCH).bit_length() - 1
    in_bits = (QB // STRETCH).bit_length() - 1
    block_bits = stretch_bits - in_bits
    levels = level_codes.shape[0]
    rows = rows_all // groups
    chips = groups // CORES
    spans = [STRETCH] + [STRETCH << j for j in range(levels - 1)]
    factors = [1.0 / 128.0 / math.sqrt(HEAD_DIM * span) for span in spans]
    n_b = rows_all // QB
    hbm = pl.BlockSpec(memory_space=pl.ANY)
    dma = pltpu.SemaphoreType.DMA
    n_w = (chips - 1) * (4 * CHUNKS + 4) + 1
    n_a = groups * (rows // QB) * heads
    return pl.pallas_call(
        functools.partial(kernel, (groups, seq_bits, block_bits, in_bits, factors)),
        out_shape=jax.ShapeDtypeStruct((rows, depth), BF16),
        in_specs=[hbm, hbm, hbm, hbm, hbm, pl.BlockSpec(memory_space=pltpu.SMEM)],
        out_specs=hbm,
        scratch_shapes=[
            pltpu.VMEM((rows_all, depth), BF16),
            pltpu.VMEM((2, depth, 4, pw), BF16),
            pltpu.VMEM((QUARTERS, width // QUARTERS, depth), jnp.int32),
            pltpu.VMEM((groups, width, depth), BF16),
            pltpu.VMEM((pairs, rows_all, 2 * pw), BF16),
            pltpu.VMEM((pairs, rows_all, pw), BF16),
            pltpu.VMEM((pairs, rows_all, pw), F32),
            pltpu.VMEM((rows_all, width), BF16),
            pltpu.VMEM((groups, rows, width), BF16),
            pltpu.VMEM((2 * n_b, heads, HEAD_DIM, HEAD_DIM), BF16),
            pltpu.VMEM((heads, HEAD_DIM, HEAD_DIM), F32),
            pltpu.VMEM((seq_bits, heads, HEAD_DIM, HEAD_DIM), BF16),
            pltpu.VMEM((seq_bits, heads, HEAD_DIM, HEAD_DIM), BF16),
            pltpu.VMEM((in_bits, QB // 2, QB // 2), F32),
            pltpu.VMEM((rows, depth), F32),
            pltpu.VMEM((rows, depth), BF16),
            pltpu.VMEM(level_codes.shape, jnp.int32),
            pltpu.VMEM((1, width), F32),
            dma((4,)), dma((2, 4)), dma((QUARTERS,)), dma((2,)), dma((rows // QB,)),
            dma((n_w,)), dma((n_w,)),
            dma((n_a,)), dma((n_a,)),
            dma((seq_bits, heads)), dma((seq_bits, heads)),
        ]
        + [pltpu.VMEM((2, depth, 2 * pw), BF16)] * pairs,
        compiler_params=pltpu.CompilerParams(
            collective_id=0, has_side_effects=True, vmem_limit_bytes=67043328
        ),
        name="layer",
    )(tokens, w_proj, w_codes, gain.reshape(1, width), level_codes, block_exponent)


def solution(mesh):
    placed = (
        P("seq", None),
        P(None, None, "mp"),
        P("mp"),
        P(None, "mp", "seq"),
        P("mp", None),
        P("mp", None),
    )
    return jax.shard_map(
        body, mesh=mesh, in_specs=placed, out_specs=P(("seq", "mp"), None), check_vma=False
    )
```

```python
import functools
import math

import jax
import jax.numpy as jnp
from jax import lax
from jax.experimental import pallas as pl
from jax.experimental.pallas import tpu as pltpu
from jax.sharding import PartitionSpec as P

HEAD_DIM = 128
STRETCH = 64
BLOCK = 128
CORES = 2
QB = 256
QUARTERS = 4
CHUNKS = 4
MESH = pl.DeviceIdType.MESH
F32 = jnp.float32
BF16 = jnp.bfloat16


def dot(a, b):
    return jnp.dot(a, b, preferred_element_type=F32)


def dot_nt(a, b):
    return lax.dot_general(a, b, (((1,), (1,)), ((), ())), preferred_element_type=F32)


def dot_tn(a, b):
    return lax.dot_general(a, b, (((0,), (0,)), ((), ())), preferred_element_type=F32)


def kernel(
    cfg,
    tok_hbm, w_hbm, codes_hbm, gain_hbm, lw_hbm, scale_ref,
    outv,
    tok, wstage, cstage, wfull, kv, q, gate, att, attr, local, tot, snd, rcv, masks, acc,
    lw_ref, gain_ref,
    tok_sem, w_sem, c_sem, in_sem, ws_sem, wr_sem, as_sem, ar_sem, ss_sem, sr_sem,
    *wh,
):
    groups, seq_bits, block_bits, in_bits, factors = cfg
    rows_all, depth = tok.shape
    pairs = len(wh)
    heads, width = tot.shape[0], att.shape[1]
    hp = heads // pairs
    pw = hp * HEAD_DIM
    rows = rows_all // groups
    chips = groups // CORES
    n_parts = rows // QB
    n_b = rows_all // QB
    seq = lax.axis_index("seq")
    mp = lax.axis_index("mp")
    x = mp // CORES
    c = mp % CORES
    bit0 = seq % 2
    bit1 = (seq // 2) % 2

    def peer(ix, kc):
        return ((x + ix) % chips) * CORES + (c + kc) % CORES

    def source(ix, kc):
        return ((x - ix + chips) % chips) * CORES + (c - kc + CORES) % CORES

    def seq_peer(j):
        bit = (seq // 2**j) % 2
        return seq + 2**j - bit * 2 ** (j + 1)

    mine = bit1 * 2 + bit0
    over0 = bit1 * 2 + 1 - bit0
    over1 = (1 - bit1) * 2 + bit0
    over01 = (1 - bit1) * 2 + 1 - bit0

    crows = width // QUARTERS
    n_t = 4
    tb = rows_all // n_t
    wrows = depth // n_t

    def code_piece(i):
        return (mine + i) % QUARTERS

    def c_copy(i):
        at = pl.ds(pl.multiple_of(code_piece(i) * crows, crows), crows)
        return pltpu.make_async_copy(codes_hbm.at[at], cstage.at[i], c_sem.at[i])

    def w_copy(h, i):
        at = pl.ds(i * wrows, wrows)
        cols = pl.ds(h * pw, pw)
        return pltpu.make_async_copy(
            w_hbm.at[at, :, cols], wstage.at[h % 2, at], w_sem.at[h % 2, i]
        )

    def tok_copy(i):
        at = pl.ds(pl.multiple_of(i * tb, tb), tb)
        return pltpu.make_async_copy(tok_hbm.at[at], tok.at[at], tok_sem.at[i])

    c_copy(0).start()
    for i in range(n_t):
        w_copy(0, i).start()
    tok_copy(0).start()
    tok_copy(1).start()
    if pairs > 1:
        for i in range(n_t):
            w_copy(1, i).start()
    tok_copy(2).start()
    tok_copy(3).start()
    for i in range(1, QUARTERS):
        c_copy(i).start()
    lw_copy = pltpu.make_async_copy(lw_hbm, lw_ref, in_sem.at[0])
    gain_copy = pltpu.make_async_copy(gain_hbm, gain_ref, in_sem.at[1])
    lw_copy.start()
    gain_copy.start()

    barrier = pltpu.get_barrier_semaphore()
    for r in range(1, groups):
        pl.semaphore_signal(
            barrier, inc=1, device_id=(seq, peer(r // CORES, r % CORES)), device_id_type=MESH
        )
    for j in range(seq_bits):
        pl.semaphore_signal(barrier, inc=1, device_id=(seq_peer(j), mp), device_id_type=MESH)

    def decode(i, start, size):
        piece = code_piece(i)
        codes = cstage[i, pl.ds(start, size)]
        whole = ((codes & 7) | 8) << ((codes >> 3) & 15)
        value = whole.astype(F32)
        value = jnp.where(codes >= 128, -value, value)
        at = pl.ds(pl.multiple_of(piece * crows + start, 16), size)
        block = piece * crows // BLOCK
        for k in range(depth // BLOCK):
            scale = jnp.left_shift(jnp.int32(1), scale_ref[block, k] + 16).astype(F32) * 2.0**-26
            cols = slice(k * BLOCK, (k + 1) * BLOCK)
            wfull[mp, at, cols] = (value[:, cols] * scale).astype(BF16)

    def relayout(p, which, start, size):
        at = pl.ds(pl.multiple_of(start, size), size)
        one, two = ((1, 2), (0, 3))[which]
        piece = jnp.swapaxes(wstage[p % 2, at], 0, 1)
        wh[p][which, at, :pw] = piece[one]
        wh[p][which, at, pw:] = piece[two]

    csize = crows // CHUNKS

    def w_send(k, shard, start, size, seq_to, mp_to):
        at = pl.ds(pl.multiple_of(start, 16), size)
        return pltpu.make_async_remote_copy(
            src_ref=wfull.at[shard, at], dst_ref=wfull.at[shard, at],
            send_sem=ws_sem.at[k], recv_sem=wr_sem.at[k],
            device_id=(seq_to, mp_to), device_id_type=MESH,
        )

    n_x = chips - 1
    per = 4 * CHUNKS + 4

    def slot(ix, kind, ch):
        return (ix - 1) * per + kind * CHUNKS + ch

    def x_part(ix, ch, shard):
        return w_send(slot(ix, 0, ch), shard, mine * crows + ch * csize, csize, seq, peer(ix, 0))

    def y_part(ix, ch, quarter):
        at = quarter * crows + ch * csize
        return w_send(slot(ix, 1, ch), source(ix, 0), at, csize, seq_peer(0), mp)

    def z_part(ix, ch, quarter):
        at = quarter * crows + ch * csize
        return w_send(slot(ix, 2, ch), source(ix, 0), at, csize, seq_peer(1), mp)

    def d_part(ix, ch, quarter):
        at = quarter * crows + ch * csize
        return w_send(slot(ix, 3, ch), source(ix, 0), at, csize, seq_peer(0), mp)

    def core_part(ix, n, kc):
        quarter = (mine, over0, over1, over01)[n]
        k = slot(ix, 4, 0) + n
        return w_send(k, source(ix, kc), quarter * crows, crows, seq, peer(0, 1))

    def own_part(shard):
        return w_send(n_x * per, shard, 0, width, seq, peer(0, 1))

    remote = range(1, chips)

    def core_send(n):
        for ix in remote:
            core_part(ix, n, 0).start()

    def x_relay(ch):
        for ix in remote:
            x_part(ix, ch, source(ix, 0)).wait_recv()
            y_part(ix, ch, mine).start()
        if ch == CHUNKS - 1:
            core_send(0)

    def z_start(ch):
        for ix in remote:
            z_part(ix, ch, mine).start()

    def z_relay(ch):
        for ix in remote:
            z_part(ix, ch, over1).wait_recv()
            d_part(ix, ch, over1).start()
        if ch == CHUNKS - 1:
            core_send(2)

    def y_done():
        for ix in remote:
            for ch in range(CHUNKS):
                y_part(ix, ch, over0).wait_recv()
        core_send(1)

    def d_done():
        for ix in remote:
            for ch in range(CHUNKS):
                d_part(ix, ch, over01).wait_recv()
        core_send(3)

    def part_of(h, which):
        lo = which * pw + h % hp * HEAD_DIM
        return slice(lo, lo + HEAD_DIM)

    def states(h):
        level = []
        for b in range(n_b):
            at = pl.ds(b * QB, QB)
            level.append(dot_tn(kv[h // hp, at, part_of(h, 1)], kv[h // hp, at, part_of(h, 0)]))
        base = 0
        while len(level) > 1:
            for b, state in enumerate(level):
                local[base + b, h] = state.astype(BF16)
            base += len(level)
            level = [level[2 * b] + level[2 * b + 1] for b in range(len(level) // 2)]
        tot[h] = level[0]
        snd[0, h] = level[0].astype(BF16)

    def s_send(j, h):
        return pltpu.make_async_remote_copy(
            src_ref=snd.at[j, h], dst_ref=rcv.at[j, h],
            send_sem=ss_sem.at[j, h], recv_sem=sr_sem.at[j, h],
            device_id=(seq_peer(j), mp), device_id_type=MESH,
        )

    progress = [0] * heads

    def exchange(h):
        j = progress[h]
        s_send(j, h).wait_recv()
        if j + 1 < seq_bits:
            total = tot[h] + rcv[j, h].astype(F32)
            tot[h] = total
            snd[j + 1, h] = total.astype(BF16)
            s_send(j + 1, h).start()
        progress[h] += 1

    def advance(p, upto):
        for h in range(p * hp, (p + 1) * hp) if p < pairs else ():
            if progress[h] < min(upto, seq_bits - 1):
                exchange(h)

    def complete(h):
        while progress[h] < seq_bits:
            exchange(h)

    def query(p, first, last, after=None):
        @pl.loop(first, last)
        def _(step):
            r = groups - 1 - step
            owner = peer(r // CORES, r % CORES)
            at = pl.ds(pl.multiple_of(owner * rows, rows), rows)
            both = dot(tok[at, :], wh[p][1])
            q[p, at, :] = both[:, :pw].astype(BF16)
            g = both[:, pw:]
            gain = gain_ref[:, p * pw : (p + 1) * pw]
            gate[p, at, :] = g / (1.0 + jnp.exp(-g)) * gain
            if after:
                pl.when(step == first)(after)

    def a_send(r, target, part, h):
        at = pl.ds(pl.multiple_of(target * rows + part * QB, QB), QB)
        to = pl.ds(pl.multiple_of(part * QB, QB), QB)
        cols = pl.ds(h * HEAD_DIM, HEAD_DIM)
        k = (r * n_parts + part) * heads + h
        return pltpu.make_async_remote_copy(
            src_ref=att.at[at, cols], dst_ref=attr.at[mp, to, cols],
            send_sem=as_sem.at[k], recv_sem=ar_sem.at[k],
            device_id=(seq, target), device_id_type=MESH,
        )

    def a_wait(r, part, h):
        src = source(r // CORES, r % CORES)
        to = pl.ds(part * QB, QB)
        cols = pl.ds(h * HEAD_DIM, HEAD_DIM)
        k = (r * n_parts + part) * heads + h
        pltpu.make_async_remote_copy(
            src_ref=attr.at[src, to, cols], dst_ref=attr.at[src, to, cols],
            send_sem=as_sem.at[k], recv_sem=ar_sem.at[k],
            device_id=(seq, src), device_id_type=MESH,
        ).wait_recv()

    unit = 2
    hb = QB // 2
    n_in = 1 + in_bits

    def attend_block(h, b):
        cols = slice(h * HEAD_DIM, (h + 1) * HEAD_DIM)
        at = pl.ds(pl.multiple_of(b * QB, QB), QB)
        qh = q[h // hp, at, part_of(h, 0)]

        def weight(level):
            return lw_ref[level, h : h + 1, at].astype(F32) * factors[level]

        scores = dot_nt(kv[h // hp, at, part_of(h, 0)], qh)

        def corner(lo):
            side = slice(lo, lo + hb)
            mix = weight(0)[:, side] * masks[0]
            for j in range(in_bits - 1):
                mix = mix + weight(1 + j)[:, side] * masks[1 + j]
            return (scores[side, side] * mix).astype(BF16)

        upper = (scores[:hb, hb:] * weight(in_bits)[:, hb:]).astype(BF16)
        probs = jnp.concatenate(
            [
                jnp.concatenate([corner(0), upper], 1),
                jnp.concatenate([jnp.zeros((hb, hb), BF16), corner(hb)], 1),
            ],
            0,
        )
        qt = qh.astype(F32).T
        left = []
        right = []
        base = 0
        for j in range(block_bits):
            node = b // 2**j
            bit = node % 2
            right.append((qt * (weight(n_in + j) * bit.astype(F32))).astype(BF16))
            left.append(local[base + node - bit, h])
            base += n_b >> j
        for j in range(seq_bits):
            bit = (seq // 2**j) % 2
            right.append((qt * (weight(n_in + block_bits + j) * bit.astype(F32))).astype(BF16))
            left.append(rcv[j, h])
        memory = dot_tn(kv[h // hp, at, part_of(h, 1)], probs) + dot(
            jnp.concatenate(left, 1), jnp.concatenate(right, 0)
        )
        mean = jnp.mean(memory * memory, axis=0, keepdims=True)
        normed = (memory * lax.rsqrt(mean + 1e-06)).T
        att[at, cols] = (normed * gate[h // hp, at, part_of(h, 0)]).astype(BF16)

    def attend(p, first, last):
        pair = range(p * hp, (p + 1) * hp)
        span = last - first

        @pl.loop(0, n_parts * span // unit)
        def _(i):
            todo = []
            for k in range(unit):
                n = i * unit + k
                r = groups - 1 - first - n % span
                todo.append((r, peer(r // CORES, r % CORES), n // span))
            for r, owner, part in todo:
                for h in pair:
                    attend_block(h, owner * n_parts + part)
            for r, owner, part in todo:
                @pl.when(r > 0)
                def _():
                    for h in pair:
                        a_send(r, owner, part, h).start()

    nb = min(512, depth)

    for i in range(n_t):
        w_copy(0, i).wait()
        relayout(0, 0, i * wrows, wrows)

    t = lax.broadcasted_iota(jnp.int32, (hb, hb), 1)
    s = lax.broadcasted_iota(jnp.int32, (hb, hb), 0)
    tc = t // STRETCH
    sc = s // STRETCH
    masks[0] = jnp.where((tc == sc) & (s <= t), 1.0, 0.0).astype(F32)
    for j in range(in_bits - 1):
        hit = ((tc // 2**j) % 2 == 1) & (sc // 2**j == tc // 2**j - 1)
        masks[j + 1] = jnp.where(hit, 1.0, 0.0).astype(F32)

    moves = {}
    for ch in range(CHUNKS):
        moves["x", ch] = functools.partial(x_relay, ch)
    for ch in range(CHUNKS):
        moves["z", ch] = functools.partial(z_start, ch)
    moves["y", 0] = y_done
    for ch in range(CHUNKS):
        moves["zr", ch] = functools.partial(z_relay, ch)
    moves["d", 0] = d_done

    def move(name, ch=0):
        step = moves.pop((name, ch), None)
        if step:
            step()

    half = n_t // 2
    sub = crows // n_t
    for p in range(pairs):
        last = p + 1 == pairs
        now = range(1, QUARTERS) if last else ()
        for i in now:
            c_copy(i).wait()
        if p == 0:
            c_copy(0).wait()

        def project(i):
            at = pl.ds(pl.multiple_of(i * tb, tb), tb)
            kv[p, at, :] = dot(tok[at, :], wh[p][0]).astype(BF16)
            for piece in now:
                decode(piece, i * sub, sub)

        def rework(other, which, i):
            for k in range(4):
                relayout(other, which, i * 2 * wrows + k * wrows // 2, wrows // 2)

        @pl.loop(0, half)
        def _(i):
            if p == 0:
                tok_copy(i).wait()
                decode(0, i * (crows // half), crows // half)
            project(i)
            if p > 0:
                rework(p - 1, 1, i)

        if p == 0:
            pl.semaphore_wait(barrier, groups - 1 + seq_bits)
            for ch in range(CHUNKS):
                for ix in remote:
                    x_part(ix, ch, mp).start()
        else:
            advance(p - 1, 1)
            move("x", 0)
            move("z", 0)
        if not last:
            for i in range(n_t):
                w_copy(p + 1, i).wait()

        @pl.loop(half, n_t)
        def _(i):
            if p == 0:
                tok_copy(i).wait()
            project(i)
            if last:
                rework(p, 1, i - half)
            else:
                rework(p + 1, 0, i - half)

        for h in range(p * hp, (p + 1) * hp):
            states(h)
            s_send(0, h).start()
        if p > 0:
            advance(p - 1, 2)
            for ch in (1, 2):
                move("x", ch)
                move("z", ch)
    own_part(mp).start()

    lw_copy.wait()
    gain_copy.wait()
    n_far = groups - CORES
    query(0, 0, n_far)
    for ch in range(CHUNKS):
        move("x", ch)
        move("z", ch)
    move("zr", 0)
    if pairs > 1:
        query(1, 0, n_far // 2)
        advance(1, 1)
    move("zr", 1)
    for h in range(hp):
        complete(h)
    attend(0, 0, n_far)
    if pairs > 1:
        query(1, n_far // 2, n_far)
        advance(1, 2)
    move("zr", 2)
    query(0, n_far, groups)
    move("y")
    move("zr", 3)
    if pairs > 1:
        query(1, n_far, groups)
        for h in range(hp, heads):
            complete(h)
        attend(1, 0, n_far)
    move("d")
    attend(0, n_far, groups)
    if pairs > 1:
        attend(1, n_far, groups)

    own = pl.ds(pl.multiple_of(mp * rows, rows), rows)
    partner = source(0, 1)
    for part in range(n_parts):
        for h in range(heads):
            a_wait(1, part, h)
    own_part(partner).wait_recv()

    @pl.loop(0, depth // nb)
    def _(i):
        cols = pl.ds(pl.multiple_of(i * nb, nb), nb)
        acc[:, cols] = dot(att[own, :], wfull[mp, :, cols]) + dot(
            attr[partner], wfull[partner, :, cols]
        )

    for name, ch in list(moves):
        move(name, ch)
    for ix in remote:
        for n in range(4):
            core_part(ix, n, 1).wait_recv()

    early = heads // 2
    cut = early * HEAD_DIM
    far = range(CORES, groups)
    for r in far:
        for part in range(n_parts):
            for h in range(early):
                a_wait(r, part, h)

    def far_sum(at, ks, cols):
        value = acc[at, cols]
        for r in far:
            src = source(r // CORES, r % CORES)
            value = value + dot(attr[src, at, ks], wfull[src, ks, cols])
        return value

    @pl.loop(0, depth // nb)
    def _(i):
        cols = pl.ds(pl.multiple_of(i * nb, nb), nb)
        acc[:, cols] = far_sum(slice(0, rows), slice(0, cut), cols)

    for part in range(n_parts):
        for r in far:
            for h in range(early, heads):
                a_wait(r, part, h)
        at = slice(part * QB, (part + 1) * QB)

        @pl.loop(0, depth // nb)
        def _(i):
            cols = pl.ds(pl.multiple_of(i * nb, nb), nb)
            outv[at, cols] = far_sum(at, slice(cut, width), cols).astype(BF16)


    own_part(mp).wait_send()
    for ix in remote:
        for ch in range(CHUNKS):
            x_part(ix, ch, mp).wait_send()
            y_part(ix, ch, mine).wait_send()
            z_part(ix, ch, mine).wait_send()
            d_part(ix, ch, over1).wait_send()
        for n in range(4):
            core_part(ix, n, 0).wait_send()
    for j in range(seq_bits):
        for h in range(heads):
            s_send(j, h).wait_send()
    for r in range(1, groups):
        for part in range(n_parts):
            for h in range(heads):
                a_send(r, peer(r // CORES, r % CORES), part, h).wait_send()


def body(tokens, w_proj, gain, level_codes, w_codes, block_exponent):
    rows_all, depth = tokens.shape
    width = w_proj.shape[2]
    heads = width // HEAD_DIM
    pw = 2 * HEAD_DIM
    pairs = width // pw
    groups = lax.axis_size("mp")
    seq_size = lax.axis_size("seq")
    seq_bits = seq_size.bit_length() - 1
    stretch_bits = (rows_all // STRETCH).bit_length() - 1
    in_bits = (QB // STRETCH).bit_length() - 1
    block_bits = stretch_bits - in_bits
    levels = level_codes.shape[0]
    rows = rows_all // groups
    chips = groups // CORES
    spans = [STRETCH] + [STRETCH << j for j in range(levels - 1)]
    factors = [1.0 / 128.0 / math.sqrt(HEAD_DIM * span) for span in spans]
    n_b = rows_all // QB
    hbm = pl.BlockSpec(memory_space=pl.ANY)
    dma = pltpu.SemaphoreType.DMA
    n_w = (chips - 1) * (4 * CHUNKS + 4) + 1
    n_a = groups * (rows // QB) * heads
    return pl.pallas_call(
        functools.partial(kernel, (groups, seq_bits, block_bits, in_bits, factors)),
        out_shape=pltpu.VMEM((rows, depth), BF16),
        in_specs=[hbm, hbm, hbm, hbm, hbm, pl.BlockSpec(memory_space=pltpu.SMEM)],
        out_specs=pl.BlockSpec(memory_space=pltpu.VMEM),
        scratch_shapes=[
            pltpu.VMEM((rows_all, depth), BF16),
            pltpu.VMEM((2, depth, 4, pw), BF16),
            pltpu.VMEM((QUARTERS, width // QUARTERS, depth), jnp.int32),
            pltpu.VMEM((groups, width, depth), BF16),
            pltpu.VMEM((pairs, rows_all, 2 * pw), BF16),
            pltpu.VMEM((pairs, rows_all, pw), BF16),
            pltpu.VMEM((pairs, rows_all, pw), F32),
            pltpu.VMEM((rows_all, width), BF16),
            pltpu.VMEM((groups, rows, width), BF16),
            pltpu.VMEM((2 * n_b, heads, HEAD_DIM, HEAD_DIM), BF16),
            pltpu.VMEM((heads, HEAD_DIM, HEAD_DIM), F32),
            pltpu.VMEM((seq_bits, heads, HEAD_DIM, HEAD_DIM), BF16),
            pltpu.VMEM((seq_bits, heads, HEAD_DIM, HEAD_DIM), BF16),
            pltpu.VMEM((in_bits, QB // 2, QB // 2), F32),
            pltpu.VMEM((rows, depth), F32),
            pltpu.VMEM(level_codes.shape, jnp.int32),
            pltpu.VMEM((1, width), F32),
            dma((4,)), dma((2, 4)), dma((QUARTERS,)), dma((2,)),
            dma((n_w,)), dma((n_w,)),
            dma((n_a,)), dma((n_a,)),
            dma((seq_bits, heads)), dma((seq_bits, heads)),
        ]
        + [pltpu.VMEM((2, depth, 2 * pw), BF16)] * pairs,
        compiler_params=pltpu.CompilerParams(
            collective_id=0, has_side_effects=True, vmem_limit_bytes=60 * 2**20
        ),
        name="layer",
    )(tokens, w_proj, w_codes, gain.reshape(1, width), level_codes, block_exponent)


def solution(mesh):
    placed = (
        P("seq", None),
        P(None, None, "mp"),
        P("mp"),
        P(None, "mp", "seq"),
        P("mp", None),
        P("mp", None),
    )
    return jax.shard_map(
        body, mesh=mesh, in_specs=placed, out_specs=P(("seq", "mp"), None), check_vma=False
    )
```
